256 devices in a mesh: row: 32 (over y, z), col: 8 (over x, core).
Axes of the slice: x: 4, y: 4, z: 8, core: 2. Of those that a mesh axis runs over, the one named last changes fastest.
Arguments:
- responses: bfloat16 [4096, 2, 3, 2048], P(('col', 'row')), may hold values from -6 to 6
- labels: int32 [2048], replicated, may hold values from 0 to 15
- conductivity: float32 [16], replicated, may hold values from 0.05 to 2
- permittivity: float32 [16], replicated, may hold values from 0.1 to 1.6
Outputs:
- noise_cov: float32 [2, 4096, 4096], P(None, 'row', 'col')
- energy_gram: float32 [2, 4096, 4096], P(None, 'row', 'col')
The draws below stay inside these ranges and needn't reach their ends.
All inputs are finite; a program needn't handle non-finite values.
Results may differ from the reference program's by a relative error of at most 0.0021.
Values may be sent and summed in bfloat16 or wider, within the bound.
No kernel may reach another device: no remote copies, remote signals or barrier semaphores. Data moves between devices by JAX's collectives and lax.ppermute only.
A program may use at most 128 MiB of HBM per device.

```python
import math
import jax
import jax.numpy as jnp
from jax import lax

NB = 4096
NV = 2048
NT = 16


def touch_ends(drawn, rng, least, high):
    extent = drawn.shape
    spot = [jax.random.randint(jax.random.fold_in(rng, axis), (), 0, extent[axis]) for axis in range(len(extent))]
    drawn = drawn.at[tuple(spot)].set(least)
    longest = extent.index(max(extent))
    spot[longest] = (spot[longest] + 1) % extent[longest]
    return drawn.at[tuple(spot)].set(high)


def level_of(own_key, dims, split, low, high):
    factor_of = 1.0
    for dim, parts in split:
        draws = jax.random.uniform(jax.random.fold_in(jax.random.fold_in(own_key, 6), dim), (parts,), jnp.float32, low / len(split), high / len(split))
        factor_of = factor_of * jnp.repeat(jnp.exp(draws), dims[dim] // parts).reshape((-1,) + (1,) * (len(dims) - 1 - dim))
    return factor_of


def bell_draw(own_key, dims, deviation, limit, shards=(), kind=jnp.bfloat16):
    loudness = level_of(own_key, dims, shards, -0.22, 0.18) if shards else 1.0
    entries = jax.random.normal(own_key, dims, jnp.float32) * deviation * loudness
    return jnp.minimum(jnp.maximum(entries, -limit), limit).astype(kind)


def setup_inputs(seed: int = 0) -> dict:
    streams_of = jax.random.split(jax.random.key(seed), 5)
    return {
        "responses": bell_draw(streams_of[0], (NB, 2, 3, NV), 1.0, 6.0, ((0, 256),)),
        "labels": touch_ends(jax.random.randint(streams_of[1], (NV,), 0, NT), jax.random.fold_in(streams_of[1], 1), 0, NT - 1).astype(jnp.int32),
        "conductivity": jnp.clip(jnp.exp(jax.random.uniform(streams_of[2], (NT,), jnp.float32, math.log(0.05), math.log(2.0))), 0.05, 2.0),
        "permittivity": jnp.clip(jnp.exp(jax.random.uniform(streams_of[3], (NT,), jnp.float32, math.log(0.1), math.log(1.6))), 0.1, 1.6),
    }


def reference(responses, labels, conductivity, permittivity):
    scale_factor = 1.0 / jnp.sqrt(jnp.float32(6 * NV))
    sig_w = conductivity[labels].astype(jnp.float32) * scale_factor
    eps_w = permittivity[labels].astype(jnp.float32) * scale_factor
    fields = responses.astype(jnp.float32)
    right_flat = responses.reshape(NB, 6 * NV)

    def weighted(weight_vec):
        scaled = fields * weight_vec[None, None, None, :]
        crossed = jnp.concatenate([-scaled[:, 1:2], scaled[:, 0:1]], axis=1)
        plain_flat = scaled.astype(jnp.bfloat16).reshape(NB, 6 * NV)
        cross_flat = crossed.astype(jnp.bfloat16).reshape(NB, 6 * NV)
        real_part = lax.dot_general(plain_flat, right_flat, (((1,), (1,)), ((), ())), preferred_element_type=jnp.float32)
        imag_part = lax.dot_general(cross_flat, right_flat, (((1,), (1,)), ((), ())), preferred_element_type=jnp.float32)
        return jnp.stack([real_part, imag_part])
    return (weighted(sig_w), weighted(eps_w))
```

```python
import jax
import jax.numpy as jnp
from jax import lax
from jax.experimental import pallas as pl
from jax.experimental.pallas import tpu as pltpu
from jax.sharding import PartitionSpec as P

NY, NZ, NX, NC = 4, 8, 4, 2
NQ = 512
KQ = 6 * NQ
BF = jnp.bfloat16
F32 = jnp.float32
VMEM_LIMIT = 56 * 1024 * 1024

BATCHES = ((0, 7, 1), (6, 2), (5, 3, 4))


def row_permute(v, move):
    pairs = []
    for y in range(NY):
        for z in range(NZ):
            y2, z2 = move(y, z)
            pairs.append((y * NZ + z, y2 % NY * NZ + z2 % NZ))
    return lax.ppermute(v, "row", pairs)


def col_permute(v, move):
    pairs = []
    for x in range(NX):
        for c in range(NC):
            x2, c2 = move(x, c)
            pairs.append((x * NC + c, x2 % NX * NC + c2 % NC))
    return lax.ppermute(v, "col", pairs)


def all_permute(v, move):
    pairs = []
    for y in range(NY):
        for z in range(NZ):
            for x in range(NX):
                for c in range(NC):
                    y2, z2, x2, c2 = move(y, z, x, c)
                    pairs.append((((y * NZ + z) * NX + x) * NC + c, ((y2 * NZ + z2) * NX + x2) * NC + c2))
    return lax.ppermute(v, ("row", "col"), pairs)


def pick(stack, i):
    return lax.dynamic_index_in_dim(stack, i, 0, keepdims=False)


def prep_kernel(pos_ref, w_ref, *refs):
    ins, out_ref = refs[:-1], refs[-1]
    y, c = pos_ref[0], pos_ref[1]
    half = len(ins) // 2
    for lane in range(2):
        lane_row = 64 * (c if lane == 0 else 1 - c)
        t = 0
        for ref in ins[lane * half:(lane + 1) * half]:
            for j in range(ref.shape[0]):
                off = pl.multiple_of(lane_row + 16 * lax.rem(y - t + NY, NY), 16)
                for m in range(6):
                    v = ref[j, m].astype(F32)
                    for k in range(2):
                        out_ref[k, pl.ds(off, 16), m * NQ:(m + 1) * NQ] = (v * w_ref[k:k + 1]).astype(BF)
                t += 1


def prep(pos, w, own, other):
    args = (*own, *other)
    return pl.pallas_call(
        prep_kernel,
        out_shape=jax.ShapeDtypeStruct((2, 128, KQ), BF),
        in_specs=[pl.BlockSpec(memory_space=pltpu.SMEM)] + [pl.BlockSpec(memory_space=pltpu.VMEM)] * (1 + len(args)),
        out_specs=pl.BlockSpec(memory_space=pltpu.VMEM),
        compiler_params=pltpu.CompilerParams(vmem_limit_bytes=VMEM_LIMIT),
        name="weigh",
    )(pos, w, *args)


def batch_kernel(n, counts, pos_ref, *refs):
    npieces = len(counts)
    pieces = refs[:npieces]
    lhs = refs[npieces:npieces + 4]
    outs = refs[npieces + 4:npieces + 8]
    rhs, left, sems = refs[npieces + 8:]
    y = pos_ref[0]
    copies = [pltpu.make_async_copy(lhs[r], left.at[r], sems.at[r]) for r in range(4)]
    for cp in copies:
        cp.start()
    nc = 64 * n
    p, t = 0, 0
    for ref, cnt in zip(pieces, counts):
        for j in range(cnt):
            ys = lax.rem(y - t + NY, NY)
            off = pl.multiple_of(ys * (16 * n) + 16 * p, 16)
            off2 = pl.multiple_of(nc + ys * (16 * n) + 16 * p, 16)
            for m in range(3):
                re = ref[j, m]
                im = ref[j, m + 3]
                rhs[pl.ds(off, 16), m * NQ:(m + 1) * NQ] = re
                rhs[pl.ds(off, 16), (m + 3) * NQ:(m + 4) * NQ] = im
                rhs[pl.ds(off2, 16), m * NQ:(m + 1) * NQ] = im
                rhs[pl.ds(off2, 16), (m + 3) * NQ:(m + 4) * NQ] = -re
            t += 1
        if t == NY:
            p, t = p + 1, 0
    for r in range(4):
        copies[r].wait()
        a = left[r].reshape(256, KQ)
        res = lax.dot_general(a, rhs[...], (((1,), (1,)), ((), ())), preferred_element_type=F32)
        s = pos_ref[2 + r]
        for k in range(4):
            @pl.when(s == k)
            def _():
                outs[k][...] = res.astype(outs[k].dtype)


def batch(pos, pieces, lhs, n):
    counts = tuple(v.shape[0] for v in pieces)
    width = 128 * n
    flops = 2 * 1024 * width * KQ
    return pl.pallas_call(
        lambda *refs: batch_kernel(n, counts, *refs),
        out_shape=[jax.ShapeDtypeStruct((256, width), F32 if k == 0 else BF) for k in range(4)],
        in_specs=[pl.BlockSpec(memory_space=pltpu.SMEM)] + [pl.BlockSpec(memory_space=pltpu.VMEM)] * len(pieces)
        + [pl.BlockSpec(memory_space=pl.ANY)] * 4,
        out_specs=[pl.BlockSpec(memory_space=pltpu.VMEM)] * 4,
        scratch_shapes=[pltpu.VMEM((width, KQ), BF), pltpu.VMEM((4, 2, 128, KQ), BF), pltpu.SemaphoreType.DMA((4,))],
        compiler_params=pltpu.CompilerParams(vmem_limit_bytes=VMEM_LIMIT),
        cost_estimate=pl.CostEstimate(flops=flops, transcendentals=0, bytes_accessed=8 << 20),
        name="partial_gram",
    )(pos, *pieces, *lhs)


def final_kernel(nb, *refs):
    parts = refs[:4 * nb]
    sels = refs[4 * nb:5 * nb]
    noise_ref, energy_ref = refs[5 * nb:]
    total = None
    for b in range(nb):
        own, *rest = parts[4 * b:4 * b + 4]
        v = own[...]
        for r in rest:
            v = v + r[...].astype(F32)
        hi = v.astype(BF)
        lo = (v - hi.astype(F32)).astype(BF)
        sel = sels[b][...]
        for u in (hi, lo):
            d = jnp.dot(u, sel, preferred_element_type=F32)
            total = d if total is None else total + d
    for e in range(2):
        noise_ref[e] = total[0:128, e * 512:(e + 1) * 512]
        energy_ref[e] = total[128:256, e * 512:(e + 1) * 512]


def final(parts, sels):
    nb = len(sels)
    shape = jax.ShapeDtypeStruct((2, 128, 512), F32)
    return pl.pallas_call(
        lambda *refs: final_kernel(nb, *refs),
        out_shape=[shape, shape],
        in_specs=[pl.BlockSpec(memory_space=pltpu.VMEM)] * (5 * nb),
        out_specs=[pl.BlockSpec(memory_space=pltpu.VMEM)] * 2,
        compiler_params=pltpu.CompilerParams(vmem_limit_bytes=VMEM_LIMIT),
        name="collect",
    )(*[v for four in parts for v in four], *sels)


def selection(offsets, z):
    n = len(offsets)
    e = jnp.arange(2)[:, None, None, None]
    ys = jnp.arange(NY)[None, :, None, None]
    zs = ((z + jnp.array(offsets, jnp.int32)) % NZ)[None, None, :, None]
    i = jnp.arange(16)[None, None, None, :]
    target = (512 * e + 128 * ys + 16 * zs + i).reshape(128 * n, 1)
    return (target == jnp.arange(1024)[None, :]).astype(BF)


def body(responses, labels, conductivity, permittivity):
    row = lax.axis_index("row")
    col = lax.axis_index("col")
    y, z = row // NZ, row % NZ
    x, c = col // NC, col % NC
    pos = jnp.stack([y, c] + [(x + r - y) % NY for r in range(4)]).astype(jnp.int32)

    classes = jnp.arange(conductivity.shape[0], dtype=jnp.int32)
    labels_q = lax.dynamic_slice_in_dim(labels, y * NQ, NQ, 0)
    onehot = (labels_q[None, :] == classes[:, None]).astype(F32)
    scale = 1.0 / jnp.sqrt(jnp.float32(6 * labels.shape[0]))
    w = jnp.stack([jnp.sum(onehot * t[:, None], axis=0) * scale for t in (conductivity, permittivity)])
    sels = [selection(o, z) for o in BATCHES]

    quarters = responses.reshape(16, 2, 3, NY, NQ).transpose(3, 1, 2, 0, 4).reshape(NY, 6, 16, NQ)

    sent = [pick(quarters, (y + s) % NY) for s in range(NY)]
    cols = jnp.stack([sent[0]] + [row_permute(sent[s], lambda a, b, s=s: (a + s, b)) for s in (1, 2, 3)])
    mine = jnp.stack([
        all_permute(pick(quarters, (z + t) % NY), lambda y, z, x, c, t=t: ((z + t) % NY, NY * c + y, x, z // 4))
        for t in range(4)
    ])

    up = row_permute(cols, lambda a, b: (a, b + 1))
    down = row_permute(cols, lambda a, b: (a, b - 1))
    left = col_permute(mine, lambda a, b: (a + 1, b))
    right = col_permute(mine, lambda a, b: (a - 1, b))
    far1 = col_permute(left[:2], lambda a, b: (a + 1, b))
    far2 = col_permute(right[2:], lambda a, b: (a - 1, b))
    up2 = row_permute(up, lambda a, b: (a, b + 1))
    down2 = row_permute(down, lambda a, b: (a, b - 1))

    def swap(v):
        return col_permute(v, lambda a, b: (a, 1 - b))

    lhs = [prep(pos, w, own, [swap(v) for v in own]) for own in ([mine], [right], [far1, far2], [left])]
    up3 = row_permute(up2, lambda a, b: (a, b + 1))
    down3 = row_permute(down2, lambda a, b: (a, b - 1))
    up4 = row_permute(up3[:2], lambda a, b: (a, b + 1))
    down4 = row_permute(down3[2:], lambda a, b: (a, b - 1))

    parts = []
    for pieces, offsets in zip(([cols, up, down], [up2, down2], [up3, down3, up4, down4]), BATCHES):
        outs = batch(pos, pieces, lhs, len(offsets))
        parts.append([outs[0]] + [row_permute(outs[s], lambda a, b, s=s: (a + s, b)) for s in (1, 2, 3)])
    return tuple(final(parts, sels))


def solution(mesh):
    in_specs = (P(("col", "row"), None, None, None), P(), P(), P())
    out_specs = (P(None, "row", "col"), P(None, "row", "col"))
    return jax.shard_map(body, mesh=mesh, in_specs=in_specs, out_specs=out_specs, check_vma=False)
```

```python
import jax
import jax.numpy as jnp
import numpy as np
from jax import lax
from jax.experimental import pallas as pl
from jax.experimental.pallas import tpu as pltpu
from jax.sharding import PartitionSpec as P

NY, NZ, NX, NC = 4, 8, 4, 2
NQ = 512
KQ = 6 * NQ
BF = jnp.bfloat16
F32 = jnp.float32
VMEM_LIMIT = 24 * 1024 * 1024
SCALE = np.float32(1) / np.sqrt(np.float32(6 * 2048))
LHS_TYPE = pltpu.VMEM((2, 128, KQ), BF)

BATCHES = ((0, 7, 1, 6), (2, 5), (3, 4))


def row_permute(v, move):
    pairs = []
    for y in range(NY):
        for z in range(NZ):
            y2, z2 = move(y, z)
            pairs.append((y * NZ + z, y2 % NY * NZ + z2 % NZ))
    return lax.ppermute(v, "row", pairs)


def col_permute(v, move):
    pairs = []
    for x in range(NX):
        for c in range(NC):
            x2, c2 = move(x, c)
            pairs.append((x * NC + c, x2 % NX * NC + c2 % NC))
    return lax.ppermute(v, "col", pairs)


def all_permute(v, move):
    pairs = []
    for y in range(NY):
        for z in range(NZ):
            for x in range(NX):
                for c in range(NC):
                    y2, z2, x2, c2 = move(y, z, x, c)
                    pairs.append((((y * NZ + z) * NX + x) * NC + c, ((y2 * NZ + z2) * NX + x2) * NC + c2))
    return lax.ppermute(v, ("row", "col"), pairs)


def pick(stack, i):
    return lax.dynamic_index_in_dim(stack, i, 0, keepdims=False)


def place():
    row, col = lax.axis_index("row"), lax.axis_index("col")
    return row // NZ, row % NZ, col // NC, col % NC


SMEM_SPEC = pl.BlockSpec(memory_space=pltpu.SMEM)
VMEM_SPEC = pl.BlockSpec(memory_space=pltpu.VMEM)


def weigh_kernel(count, tab0_ref, tab1_ref, labels_ref, *refs):
    ins, out_ref = refs[:-1], refs[-1]
    y, _, _, c = place()
    labels = labels_ref[0:1, pl.ds(pl.multiple_of(y * NQ, NQ), NQ)]
    weights = []
    for tab in (tab0_ref, tab1_ref):
        w = jnp.zeros((1, NQ), F32)
        for k in range(count):
            w = jnp.where(labels == k, tab[k], w)
        weights.append(w * SCALE)
    half = len(ins) // 2
    for lane in range(2):
        lane_row = 64 * (c if lane == 0 else 1 - c)
        t = 0
        for ref in ins[lane * half:(lane + 1) * half]:
            for j in range(ref.shape[0]):
                off = pl.multiple_of(lane_row + 16 * lax.rem(y - t + NY, NY), 16)
                for m in range(6):
                    v = ref[j, m].astype(F32)
                    for k in range(2):
                        out_ref[k, pl.ds(off, 16), m * NQ:(m + 1) * NQ] = (v * weights[k]).astype(BF)
                t += 1


def weigh(tables, labels, own, other):
    args = (*own, *other)
    count = tables[0].shape[0]
    return pl.pallas_call(
        lambda *refs: weigh_kernel(count, *refs),
        out_shape=LHS_TYPE,
        in_specs=[SMEM_SPEC] * 2 + [VMEM_SPEC] * (1 + len(args)),
        out_specs=VMEM_SPEC,
        compiler_params=pltpu.CompilerParams(vmem_limit_bytes=VMEM_LIMIT),
        cost_estimate=pl.CostEstimate(flops=4 << 20, transcendentals=0, bytes_accessed=3 << 20),
        name="weigh",
    )(*tables, labels, *args)


def batch_kernel(n, counts, *refs):
    npieces = len(counts)
    pieces = refs[:npieces]
    lhs = refs[npieces:npieces + 4]
    outs = refs[npieces + 4:npieces + 8]
    rhs = refs[npieces + 8]
    y, _, x, _ = place()
    nc = 64 * n
    p, t = 0, 0
    for ref, cnt in zip(pieces, counts):
        for j in range(cnt):
            ys = lax.rem(y - t + NY, NY)
            off = pl.multiple_of(ys * (16 * n) + 16 * p, 16)
            off2 = pl.multiple_of(nc + ys * (16 * n) + 16 * p, 16)
            for m in range(3):
                re = ref[j, m]
                im = ref[j, m + 3]
                rhs[pl.ds(off, 16), m * NQ:(m + 1) * NQ] = re
                rhs[pl.ds(off, 16), (m + 3) * NQ:(m + 4) * NQ] = im
                rhs[pl.ds(off2, 16), m * NQ:(m + 1) * NQ] = im
                rhs[pl.ds(off2, 16), (m + 3) * NQ:(m + 4) * NQ] = -re
            t += 1
        if t == NY:
            p, t = p + 1, 0
    for r in range(4):
        a = lhs[r][...].reshape(256, KQ)
        res = lax.dot_general(a, rhs[...], (((1,), (1,)), ((), ())), preferred_element_type=F32)
        s = lax.rem(x + r - y + NY, NY)
        for k in range(4):
            @pl.when(s == k)
            def _():
                outs[k][...] = res.astype(outs[k].dtype)


def batch(pieces, lhs, n):
    counts = tuple(v.shape[0] for v in pieces)
    width = 128 * n
    flops = 2 * 1024 * width * KQ
    return pl.pallas_call(
        lambda *refs: batch_kernel(n, counts, *refs),
        out_shape=[jax.ShapeDtypeStruct((256, width), F32 if k == 0 else BF) for k in range(4)],
        in_specs=[VMEM_SPEC] * (len(pieces) + 4),
        out_specs=[VMEM_SPEC] * 4,
        scratch_shapes=[pltpu.VMEM((width, KQ), BF)],
        compiler_params=pltpu.CompilerParams(vmem_limit_bytes=VMEM_LIMIT),
        cost_estimate=pl.CostEstimate(flops=flops, transcendentals=0, bytes_accessed=4 << 20),
        name="partial_gram",
    )(*pieces, *lhs)


def order_kernel(out_ref):
    _, z, _, _ = place()
    base = 0
    for offsets in BATCHES:
        n = len(offsets)
        k = lax.broadcasted_iota(jnp.int32, (64 * n, NQ), 0)
        j = lax.broadcasted_iota(jnp.int32, (64 * n, NQ), 1)
        p = (k // 16) % n
        zs = jnp.full(k.shape, lax.rem(z + offsets[0], NZ))
        for q in range(1, n):
            zs = jnp.where(p == q, lax.rem(z + offsets[q], NZ), zs)
        target = 128 * (k // (16 * n)) + 16 * zs + k % 16
        out_ref[base:base + 64 * n] = (target == j).astype(F32).astype(BF)
        base += 64 * n


def collect_kernel(nb, *refs):
    parts = refs[:4 * nb]
    order_ref, noise_ref, energy_ref = refs[4 * nb:]
    total = [None, None]
    base = 0
    for b in range(nb):
        own, *rest = parts[4 * b:4 * b + 4]
        width = own.shape[1] // 2
        sel = order_ref[base:base + width]
        base += width
        for e in range(2):
            v = own[:, e * width:(e + 1) * width]
            for r in rest:
                v = v + r[:, e * width:(e + 1) * width].astype(F32)
            hi = v.astype(BF)
            lo = (v - hi.astype(F32)).astype(BF)
            d = jnp.dot(jnp.concatenate([hi, lo], axis=0), sel, preferred_element_type=F32)
            total[e] = d if total[e] is None else total[e] + d
    for e in range(2):
        d = total[e][0:256] + total[e][256:512]
        noise_ref[e] = d[0:128]
        energy_ref[e] = d[128:256]


def collect(parts):
    nb = len(BATCHES)
    order = pl.pallas_call(
        order_kernel,
        out_shape=jax.ShapeDtypeStruct((NQ, NQ), BF),
        out_specs=VMEM_SPEC,
        compiler_params=pltpu.CompilerParams(vmem_limit_bytes=VMEM_LIMIT),
        name="order",
    )()
    shape = jax.ShapeDtypeStruct((2, 128, 512), F32)
    return pl.pallas_call(
        lambda *refs: collect_kernel(nb, *refs),
        out_shape=[shape, shape],
        in_specs=[VMEM_SPEC] * (4 * nb + 1),
        out_specs=[VMEM_SPEC] * 2,
        compiler_params=pltpu.CompilerParams(vmem_limit_bytes=VMEM_LIMIT),
        name="collect",
    )(*[v for four in parts for v in four], order)


def body(responses, labels, conductivity, permittivity):
    y, _, _, c = place()
    tables = (conductivity, permittivity)
    labels = labels.reshape(1, labels.shape[0])
    quarters = responses.reshape(16, 2, 3, NY, NQ).transpose(3, 1, 2, 0, 4).reshape(NY, 6, 16, NQ)

    def along_y(v):
        got = [pick(v, y)]
        got += [row_permute(pick(v, (y + s) % NY), lambda a, b, s=s: (a + s, b)) for s in (1, 2, 3)]
        return jnp.stack(got)

    def one_way(first, second):
        return jnp.where(c == 0, first, second)

    cols = along_y(quarters)
    moved = all_permute(quarters, lambda y, z, x, c: (z % NY, NY * c + y, x, z // NY))
    up = row_permute(cols, lambda a, b: (a, b + 1))
    down = row_permute(cols, lambda a, b: (a, b - 1))
    mine = along_y(moved)
    left = col_permute(mine, lambda a, b: (a + 1, b))
    right = col_permute(mine, lambda a, b: (a - 1, b))
    far = col_permute(one_way(left, right), lambda a, b: (a + 1 - 2 * b, b))
    up2 = row_permute(up, lambda a, b: (a, b + 1))
    down2 = row_permute(down, lambda a, b: (a, b - 1))

    def swap(v):
        return col_permute(v, lambda a, b: (a, 1 - b))

    lhs = [weigh(tables, labels, [own], [swap(own)]) for own in (mine, right, far, left)]
    up3 = row_permute(up2, lambda a, b: (a, b + 1))
    down3 = row_permute(down2, lambda a, b: (a, b - 1))
    last = all_permute(one_way(up3, down3), lambda y, z, x, c: (y, (z + 1 - 2 * c) % NZ, x, c))

    parts = []
    for pieces, offsets in zip(([cols, up, down, up2], [down2, up3], [down3, last]), BATCHES):
        outs = batch(pieces, lhs, len(offsets))
        parts.append([outs[0]] + [row_permute(outs[s], lambda a, b, s=s: (a + s, b)) for s in (2, 1, 3)])
    return tuple(collect(parts))


def solution(mesh):
    in_specs = (P(("col", "row"), None, None, None), P(), P(), P())
    out_specs = (P(None, "row", "col"), P(None, "row", "col"))
    return jax.shard_map(body, mesh=mesh, in_specs=in_specs, out_specs=out_specs, check_vma=False)
```

```python
import jax
import jax.numpy as jnp
import numpy as np
from jax import lax
from jax.experimental import pallas as pl
from jax.experimental.pallas import tpu as pltpu
from jax.sharding import PartitionSpec as P

NY, NZ, NX, NC = 4, 8, 4, 2
NQ = 512
KQ = 6 * NQ
BF = jnp.bfloat16
F32 = jnp.float32
VMEM_LIMIT = 24 * 1024 * 1024
SCALE = np.float32(1) / np.sqrt(np.float32(6 * 2048))
COST = pl.CostEstimate(flops=1, transcendentals=0, bytes_accessed=1)
SMEM_SPEC = pl.BlockSpec(memory_space=pltpu.SMEM)
VMEM_SPEC = pl.BlockSpec(memory_space=pltpu.VMEM)
PARAMS = pltpu.CompilerParams(vmem_limit_bytes=VMEM_LIMIT)

RING4 = (0, -1, 1, 2)


def place():
    row, col = lax.axis_index("row"), lax.axis_index("col")
    return row // NZ, row % NZ, col // NC, col % NC


def permute(v, move):
    pairs = []
    for y in range(NY):
        for z in range(NZ):
            for x in range(NX):
                for c in range(NC):
                    y2, z2, x2, c2 = move(y, z, x, c)
                    to = ((y2 % NY * NZ + z2 % NZ) * NX + x2 % NX) * NC + c2
                    pairs.append((((y * NZ + z) * NX + x) * NC + c, to))
    return lax.ppermute(v, ("row", "col"), pairs)


def along(axis, step):
    dy, dz, dx = ((step if axis == a else 0) for a in "yzx")
    return lambda y, z, x, c: (y + dy, z + dz, x + dx, c)


def swap(v):
    return permute(v, lambda y, z, x, c: (y, z, x, 1 - c))


def ring4(v, axis):
    half = v.shape[0] // 2
    before = permute(v, along(axis, 1))
    after = permute(v, along(axis, -1))
    far = [permute(before[:half], along(axis, 1)), permute(after[half:], along(axis, -1))]
    return [v], [before], [after], far


def weigh_kernel(count, quarter, tab0_ref, tab1_ref, labels_ref, *refs):
    ins, out_ref = refs[:-1], refs[-1]
    c = place()[3]
    labels = labels_ref[0:1, pl.ds(pl.multiple_of((2 * c + quarter) * NQ, NQ), NQ)]
    weights = []
    for tab in (tab0_ref, tab1_ref):
        w = jnp.zeros((1, NQ), F32)
        for k in range(count):
            w = jnp.where(labels == k, tab[k], w)
        weights.append(w * SCALE)
    off = 0
    for ref in ins:
        for j in range(ref.shape[0]):
            for lane in range(NC):
                for m in range(6):
                    v = ref[j, lane, m].astype(F32)
                    for k in range(2):
                        out_ref[k, off:off + 16, m * NQ:(m + 1) * NQ] = (v * weights[k]).astype(BF)
                off += 16


def weigh(tables, labels, quarter, pieces):
    count = tables[0].shape[0]
    return pl.pallas_call(
        lambda *refs: weigh_kernel(count, quarter, *refs),
        out_shape=pltpu.VMEM((2, 128, KQ), BF),
        in_specs=[SMEM_SPEC] * 2 + [VMEM_SPEC] * (1 + len(pieces)),
        out_specs=VMEM_SPEC,
        compiler_params=PARAMS,
        cost_estimate=COST,
        name="weigh",
    )(*tables, labels, *pieces)


def columns_kernel(plan, *refs):
    outs = refs[-2:]
    z = place()[1]
    for ref, (step, first) in zip(refs, plan):
        base = pl.multiple_of(16 * lax.rem(z + step + NZ, NZ), 16)
        base2 = pl.multiple_of(128 + 16 * lax.rem(z + step + NZ, NZ), 16)
        for j in range(ref.shape[0]):
            out = outs[first + j]
            for q in range(2):
                for m in range(3):
                    re, im = ref[j, q, m], ref[j, q, m + 3]
                    lo = slice(q * KQ + m * NQ, q * KQ + (m + 1) * NQ)
                    hi = slice(q * KQ + (m + 3) * NQ, q * KQ + (m + 4) * NQ)
                    out[pl.ds(base, 16), lo] = re
                    out[pl.ds(base, 16), hi] = im
                    out[pl.ds(base2, 16), lo] = im
                    out[pl.ds(base2, 16), hi] = -re


def columns(pieces, plan):
    return pl.pallas_call(
        lambda *refs: columns_kernel(plan, *refs),
        out_shape=[pltpu.VMEM((256, 2 * KQ), BF)] * NC,
        in_specs=[VMEM_SPEC] * len(pieces),
        out_specs=[VMEM_SPEC] * NC,
        compiler_params=PARAMS,
        cost_estimate=COST,
        name="columns",
    )(*pieces)


def gram_kernel(steps, carried, *refs):
    out_ref = refs[-1]
    rhs = refs[carried]
    lhs = refs[carried + 1:-1]
    y, _, x, c = place()
    out_ref[...] = refs[0][...] if carried else jnp.zeros(out_ref.shape, F32)
    for q in range(2):
        for k, step in enumerate(steps):
            a = lhs[q * len(steps) + k][...].reshape(256, KQ)
            d = lax.dot_general(a, rhs[:, q * KQ:(q + 1) * KQ], (((1,), (1,)), ((), ())), preferred_element_type=F32)
            for j, other in enumerate(RING4):
                dx, dy = (step, other) if q == 0 else (other, step)
                at = 128 * lax.rem(x + dx + NX, NX) + 16 * lax.rem(y + dy + NY, NY)
                for lane in range(NC):
                    off = pl.multiple_of(at + 64 * (c if lane == 0 else 1 - c), 16)
                    lo = 32 * j + 16 * lane
                    for k2 in range(2):
                        out_ref[k2, pl.ds(off, 16), :] += d[128 * k2 + lo:128 * k2 + lo + 16]


def gram(acc, rhs, lhs, steps):
    carried = acc is not None
    args = ([acc] if carried else []) + [rhs] + lhs
    return pl.pallas_call(
        lambda *refs: gram_kernel(steps, int(carried), *refs),
        out_shape=pltpu.VMEM((2, 512, 256), F32),
        in_specs=[VMEM_SPEC] * len(args),
        out_specs=VMEM_SPEC,
        compiler_params=PARAMS,
        cost_estimate=COST,
        name="gram",
    )(*args)


def pack_kernel(a_ref, b_ref, out_ref):
    for k in range(2):
        for f in range(NY * NZ):
            v = (a_ref[k, 16 * f:16 * f + 16] + b_ref[k, 16 * f:16 * f + 16]).astype(BF)
            for e in range(2):
                out_ref[f, 2 * k + e] = v[:, 128 * e:128 * e + 128]


def pack(a, b):
    return pl.pallas_call(
        pack_kernel,
        out_shape=jax.ShapeDtypeStruct((NY * NZ, 4, 16, 128), BF),
        in_specs=[VMEM_SPEC] * 2,
        out_specs=VMEM_SPEC,
        compiler_params=PARAMS,
        cost_estimate=COST,
        name="pack",
    )(a, b)


def assemble_kernel(in_ref, noise_ref, energy_ref):
    for y in range(NY):
        for z in range(NZ):
            for e in range(2):
                for k, out in enumerate((noise_ref, energy_ref)):
                    v = in_ref[y * NZ + z, 2 * k + e].astype(F32)
                    out[e, 16 * z:16 * z + 16, 128 * y:128 * y + 128] = v


def assemble(v):
    shape = jax.ShapeDtypeStruct((2, 128, NQ), F32)
    return pl.pallas_call(
        assemble_kernel,
        out_shape=[shape, shape],
        in_specs=[VMEM_SPEC],
        out_specs=[VMEM_SPEC] * 2,
        compiler_params=PARAMS,
        cost_estimate=COST,
        name="assemble",
    )(v)


def body(responses, labels, conductivity, permittivity):
    c = place()[3]
    tables = (conductivity, permittivity)
    labels = labels.reshape(1, labels.shape[0])
    halves = responses.reshape(16, 2, 3, 4, NQ).transpose(3, 1, 2, 0, 4).reshape(2, 2, 6, 16, NQ)

    theirs = swap(lax.dynamic_index_in_dim(halves, 1 - c, 0, keepdims=False))
    base = jnp.stack([lax.dynamic_index_in_dim(halves, c, 0, keepdims=False), theirs])

    pieces, plan = [base], [(0, 0)]
    up = down = base
    for k in (1, 2, 3):
        up, down = permute(up, along("z", 1)), permute(down, along("z", -1))
        pieces += [up, down]
        plan += [(-k, 0), (k, 0)]
    pieces += [permute(up[:1], along("z", 1)), permute(down[1:], along("z", -1))]
    plan += [(-4, 0), (4, 1)]
    rhs = columns(pieces, plan)

    def two_rings(quarter, first, second):
        ring = ring4(base[:, quarter], first)
        own = jnp.concatenate([v for part in ring for v in part]).reshape(4, NC, 6, 16, NQ)
        return [weigh(tables, labels, quarter, part) for part in ring4(own, second)]

    rows0 = two_rings(0, "y", "x")
    rows1 = two_rings(1, "x", "y")

    sums = []
    for lane in (1, 0):
        acc = gram(None, rhs[lane], rows0[:3] + rows1[:3], RING4[:3])
        acc = gram(acc, rhs[lane], rows0[3:] + rows1[3:], RING4[3:])
        sums.append(swap(acc) if lane else acc)
    packed = pack(sums[1], sums[0])
    moved = lax.all_to_all(packed, "row", 0, 0, tiled=True)
    return tuple(assemble(moved))


def solution(mesh):
    in_specs = (P(("col", "row"), None, None, None), P(), P(), P())
    out_specs = (P(None, "row", "col"), P(None, "row", "col"))
    return jax.shard_map(body, mesh=mesh, in_specs=in_specs, out_specs=out_specs, check_vma=False)
```

```python
import jax
import jax.numpy as jnp
import numpy as np
from jax import lax
from jax.experimental import pallas as pl
from jax.experimental.pallas import tpu as pltpu
from jax.sharding import PartitionSpec as P

NY, NZ, NX, NC = 4, 8, 4, 2
NQ = 512
KQ = 6 * NQ
BF = jnp.bfloat16
F32 = jnp.float32
VMEM_LIMIT = 24 * 1024 * 1024
SCALE = np.float32(1) / np.sqrt(np.float32(6 * 2048))
COST = pl.CostEstimate(flops=1, transcendentals=0, bytes_accessed=1)
SMEM_SPEC = pl.BlockSpec(memory_space=pltpu.SMEM)
VMEM_SPEC = pl.BlockSpec(memory_space=pltpu.VMEM)
PARAMS = pltpu.CompilerParams(vmem_limit_bytes=VMEM_LIMIT)

RING4 = (0, -1, 1, 2)


def place():
    row, col = lax.axis_index("row"), lax.axis_index("col")
    return row // NZ, row % NZ, col // NC, col % NC


def permute(v, move):
    pairs = []
    for y in range(NY):
        for z in range(NZ):
            for x in range(NX):
                for c in range(NC):
                    y2, z2, x2, c2 = move(y, z, x, c)
                    to = ((y2 % NY * NZ + z2 % NZ) * NX + x2 % NX) * NC + c2
                    pairs.append((((y * NZ + z) * NX + x) * NC + c, to))
    return lax.ppermute(v, ("row", "col"), pairs)


def along(axis, step):
    dy, dz, dx = ((step if axis == a else 0) for a in "yzx")
    return lambda y, z, x, c: (y + dy, z + dz, x + dx, c)


def swap(v):
    return permute(v, lambda y, z, x, c: (y, z, x, 1 - c))


def ring4(v, axis):
    half = v.shape[0] // 2
    before = permute(v, along(axis, 1))
    after = permute(v, along(axis, -1))
    far = [permute(before[:half], along(axis, 1)), permute(after[half:], along(axis, -1))]
    return [v], [before], [after], far


def weigh_kernel(count, quarter, tab0_ref, tab1_ref, labels_ref, *refs):
    ins, out_ref = refs[:-1], refs[-1]
    c = place()[3]
    labels = labels_ref[0:1, pl.ds(pl.multiple_of((2 * c + quarter) * NQ, NQ), NQ)]
    weights = []
    for tab in (tab0_ref, tab1_ref):
        w = jnp.zeros((1, NQ), F32)
        for k in range(count):
            w = jnp.where(labels == k, tab[k], w)
        weights.append(w * SCALE)
    off = 0
    for ref in ins:
        for j in range(ref.shape[0]):
            for lane in range(NC):
                for m in range(6):
                    v = ref[j, lane, m].astype(F32)
                    for k in range(2):
                        out_ref[k, off:off + 16, m * NQ:(m + 1) * NQ] = (v * weights[k]).astype(BF)
                off += 16


def weigh(tables, labels, quarter, pieces):
    count = tables[0].shape[0]
    return pl.pallas_call(
        lambda *refs: weigh_kernel(count, quarter, *refs),
        out_shape=pltpu.VMEM((2, 128, KQ), BF),
        in_specs=[SMEM_SPEC] * 2 + [VMEM_SPEC] * (1 + len(pieces)),
        out_specs=VMEM_SPEC,
        compiler_params=PARAMS,
        cost_estimate=COST,
        name="weigh",
    )(*tables, labels, *pieces)


def columns_kernel(plan, *refs):
    outs = refs[-2:]
    z = place()[1]
    for ref, (step, first) in zip(refs, plan):
        base = pl.multiple_of(16 * lax.rem(z + step + NZ, NZ), 16)
        base2 = pl.multiple_of(128 + 16 * lax.rem(z + step + NZ, NZ), 16)
        for j in range(ref.shape[0]):
            out = outs[first + j]
            for q in range(2):
                for m in range(3):
                    re, im = ref[j, q, m], ref[j, q, m + 3]
                    lo = slice(q * KQ + m * NQ, q * KQ + (m + 1) * NQ)
                    hi = slice(q * KQ + (m + 3) * NQ, q * KQ + (m + 4) * NQ)
                    out[pl.ds(base, 16), lo] = re
                    out[pl.ds(base, 16), hi] = im
                    out[pl.ds(base2, 16), lo] = im
                    out[pl.ds(base2, 16), hi] = -re


def columns(pieces, plan):
    return pl.pallas_call(
        lambda *refs: columns_kernel(plan, *refs),
        out_shape=[pltpu.VMEM((256, 2 * KQ), BF)] * NC,
        in_specs=[VMEM_SPEC] * len(pieces),
        out_specs=[VMEM_SPEC] * NC,
        compiler_params=PARAMS,
        cost_estimate=COST,
        name="columns",
    )(*pieces)


def gram_kernel(steps, carried, *refs):
    out_ref = refs[-1]
    rhs = refs[carried]
    lhs = refs[carried + 1:-1]
    y, _, x, c = place()
    out_ref[...] = refs[0][...] if carried else jnp.zeros(out_ref.shape, F32)
    for q in range(2):
        for k, step in enumerate(steps):
            a = lhs[q * len(steps) + k][...].reshape(256, KQ)
            d = lax.dot_general(a, rhs[:, q * KQ:(q + 1) * KQ], (((1,), (1,)), ((), ())), preferred_element_type=F32)
            for j, other in enumerate(RING4):
                dx, dy = (step, other) if q == 0 else (other, step)
                at = 128 * lax.rem(x + dx + NX, NX) + 16 * lax.rem(y + dy + NY, NY)
                for lane in range(NC):
                    off = pl.multiple_of(at + 64 * (c if lane == 0 else 1 - c), 16)
                    lo = 32 * j + 16 * lane
                    for k2 in range(2):
                        out_ref[k2, pl.ds(off, 16), :] += d[128 * k2 + lo:128 * k2 + lo + 16]


def gram(acc, rhs, lhs, steps):
    carried = acc is not None
    args = ([acc] if carried else []) + [rhs] + lhs
    return pl.pallas_call(
        lambda *refs: gram_kernel(steps, int(carried), *refs),
        out_shape=pltpu.VMEM((2, 512, 256), F32),
        in_specs=[VMEM_SPEC] * len(args),
        out_specs=VMEM_SPEC,
        compiler_params=PARAMS,
        cost_estimate=COST,
        name="gram",
    )(*args)


def pack_kernel(a_ref, b_ref, out_ref):
    for k in range(2):
        for f in range(NY * NZ):
            v = (a_ref[k, 16 * f:16 * f + 16] + b_ref[k, 16 * f:16 * f + 16]).astype(BF)
            for e in range(2):
                out_ref[f, 2 * k + e] = v[:, 128 * e:128 * e + 128]


def pack(a, b):
    return pl.pallas_call(
        pack_kernel,
        out_shape=jax.ShapeDtypeStruct((NY * NZ, 4, 16, 128), BF),
        in_specs=[VMEM_SPEC] * 2,
        out_specs=VMEM_SPEC,
        compiler_params=PARAMS,
        cost_estimate=COST,
        name="pack",
    )(a, b)


def assemble_kernel(in_ref, noise_ref, energy_ref):
    for y in range(NY):
        for z in range(NZ):
            for e in range(2):
                for k, out in enumerate((noise_ref, energy_ref)):
                    v = in_ref[y * NZ + z, 2 * k + e].astype(F32)
                    out[e, 16 * z:16 * z + 16, 128 * y:128 * y + 128] = v


def assemble(v):
    shape = jax.ShapeDtypeStruct((2, 128, NQ), F32)
    return pl.pallas_call(
        assemble_kernel,
        out_shape=[shape, shape],
        in_specs=[VMEM_SPEC],
        out_specs=[VMEM_SPEC] * 2,
        compiler_params=PARAMS,
        cost_estimate=COST,
        name="assemble",
    )(v)


def body(responses, labels, conductivity, permittivity):
    c = place()[3]
    tables = (conductivity, permittivity)
    labels = labels.reshape(1, labels.shape[0])
    halves = responses.reshape(16, 2, 3, 4, NQ).transpose(3, 1, 2, 0, 4).reshape(2, 2, 6, 16, NQ)

    theirs = swap(lax.dynamic_index_in_dim(halves, 1 - c, 0, keepdims=False))
    base = jnp.stack([lax.dynamic_index_in_dim(halves, c, 0, keepdims=False), theirs])

    pieces, plan = [base], [(0, 0)]
    up = down = base
    for k in (1, 2, 3):
        up, down = permute(up, along("z", 1)), permute(down, along("z", -1))
        pieces += [up, down]
        plan += [(-k, 0), (k, 0)]
    pieces += [permute(up[:1], along("z", 1)), permute(down[1:], along("z", -1))]
    plan += [(-4, 0), (4, 1)]
    rhs = columns(pieces, plan)

    def two_rings(quarter, first, second):
        ring = ring4(base[:, quarter], first)
        own = jnp.concatenate([v for part in ring for v in part]).reshape(4, NC, 6, 16, NQ)
        return [weigh(tables, labels, quarter, part) for part in ring4(own, second)]

    rows0 = two_rings(0, "y", "x")
    rows1 = two_rings(1, "x", "y")

    sums = []
    for lane in (1, 0):
        if lane:
            acc = gram(None, rhs[lane], rows0[:3] + rows1[:3], RING4[:3])
            sums.append(swap(gram(acc, rhs[lane], rows0[3:] + rows1[3:], RING4[3:])))
        else:
            sums.append(gram(None, rhs[lane], rows0 + rows1, RING4))
    packed = pack(sums[1], sums[0])
    moved = lax.all_to_all(packed, "row", 0, 0, tiled=True)
    return tuple(assemble(moved))


def solution(mesh):
    in_specs = (P(("col", "row"), None, None, None), P(), P(), P())
    out_specs = (P(None, "row", "col"), P(None, "row", "col"))
    return jax.shard_map(body, mesh=mesh, in_specs=in_specs, out_specs=out_specs, check_vma=False)
```
